512 devices in a mesh: pages: 64 (over y, z_lo, core), heads: 8 (over x, z_hi).
Axes of the slice: x: 4, y: 8, z: 8 (z_hi: 2, z_lo: 4; z = z_hi * 4 + z_lo), core: 2. Of those that a mesh axis runs over, the one named last changes fastest.
Arguments:
- candidates: bfloat16 [49152, 1024], P(('pages', 'heads')), may hold values from -6 to 6
- in_weight: bfloat16 [2, 1024, 8, 512], P(None, None, 'heads'), may hold values from -0.1875 to 0.1875
- out_weight: bfloat16 [2, 8, 128, 1024], P(None, 'heads'), may hold values from -0.1875 to 0.1875
- page_cache: bfloat16 [2, 4096, 8, 2, 32, 128], P(None, 'pages', 'heads'), may hold values from -6 to 6
- page_lists: int32 [1024, 4], P('pages'), may hold values from 0 to 4095, as said below
- hist_len: int32 [1024], P('pages'), may hold values from 1 to 128
Outputs:
- hidden_out: bfloat16 [49152, 1024], P(('pages', 'heads'))
The draws below stay inside these ranges and needn't reach their ends.
Inputs may be any that keep to these rules, and one draw needn't show every extreme that they name: `page_lists`: every page id appears in exactly one list. Page p lies on index p // 64 of pages; the requests of one index of pages list either none or exactly 2 pages that lie on any one index.
All inputs are finite; a program needn't handle non-finite values.
Results may differ from the reference program's by a relative error of at most 0.018.
Values may be sent and summed in bfloat16 or wider, within the bound.
A program may use at most 64 MiB of HBM per device.

```python
import functools
import math
import jax
import jax.numpy as jnp
from jax import lax

D = 1024
HEADS = 8
HD = 128
LAYERS = 2
PAGE = 32
MAXP = 4
REQ_DEV = 16
CPR = 48
CAND_DEV = 768
REQS = 1024
CANDS = 49152
NPAGES = 4096
N_PAGES = 64
N_HEADS = 8


def draw_page_lists(key, part):
    readers = REQS // REQ_DEV
    slot_count = REQ_DEV * MAXP
    capacity = 2 * slot_count // readers
    group_count = slot_count // capacity
    draw_keys = jax.random.split(key, 5)
    reader_shift = jax.random.permutation(draw_keys[0], readers)
    group_shift = jax.random.permutation(draw_keys[1], readers)[:group_count]
    group_order = jax.random.permutation(draw_keys[2], group_count)
    owner_offset = jax.random.randint(draw_keys[3], (readers,), 0, group_count)
    slot_keys = jax.random.split(draw_keys[4], readers)
    shuffles = jax.vmap(functools.partial(jax.random.permutation, x=slot_count))(slot_keys)
    group_of = shuffles // capacity
    within = shuffles % capacity
    owners = (reader_shift[:, None] + group_shift[group_of]) % readers
    local_pages = (group_order[group_of] * capacity + within + owner_offset[owners] * capacity) % slot_count
    page_ids = owners * slot_count + local_pages
    return page_ids.reshape(readers * REQ_DEV, MAXP).astype(jnp.int32)


def touch_ends(entries, stream_key, smallest, largest):
    spot = [jax.random.randint(jax.random.fold_in(stream_key, axis), (), 0, length) for axis, length in enumerate(entries.shape)]
    main_axis = entries.shape.index(max(entries.shape))
    neighbour = spot[:main_axis] + [(spot[main_axis] + 1) % entries.shape[main_axis]] + spot[main_axis + 1:]
    return entries.at[tuple(spot)].set(smallest).at[tuple(neighbour)].set(largest)


def block_levels(stream_key, dims, cuts, least, largest):
    loudness = 1.0
    for dim, shards_of in cuts:
        heights = jax.random.uniform(jax.random.fold_in(jax.random.fold_in(stream_key, 6), dim), (shards_of,), jnp.float32, least / len(cuts), largest / len(cuts))
        loudness = loudness * jnp.repeat(jnp.exp(heights), dims[dim] // shards_of).reshape((-1,) + (1,) * (len(dims) - 1 - dim))
    return loudness


def normal_values(rng, shape, width, most, cuts=(), held_as=jnp.bfloat16):
    loudness = block_levels(rng, shape, cuts, -0.22, 0.18) if cuts else 1.0
    result = jax.random.normal(rng, shape, jnp.float32) * width * loudness
    return jnp.minimum(jnp.maximum(result, -most), most).astype(held_as)


def setup_inputs(seed: int = 0) -> dict:
    streams_of = jax.random.split(jax.random.key(seed), 7)
    return {
        "candidates": normal_values(streams_of[0], (CANDS, D), 1.0, 6.0, ((0, 512),)),
        "in_weight": normal_values(streams_of[1], (LAYERS, D, HEADS, 4 * HD), D ** -0.5, 0.1875, ((2, 8),)),
        "out_weight": normal_values(streams_of[2], (LAYERS, HEADS, HD, D), (HEADS * HD) ** -0.5, 0.1875, ((1, 8),)),
        "page_cache": normal_values(streams_of[3], (LAYERS, NPAGES, HEADS, 2, PAGE, HD), 1.0, 6.0, ((1, 64), (2, 8))),
        "page_lists": draw_page_lists(jax.random.fold_in(streams_of[6], 71), 0),
        "hist_len": touch_ends(jax.random.randint(streams_of[5], (REQS,), 1, MAXP * PAGE + 1), jax.random.fold_in(streams_of[5], 1), 1, MAXP * PAGE).astype(jnp.int32),
    }


eps = 1e-05

def layer_norm(values):
    row_mean = lax.optimization_barrier(jnp.mean(values, -1, keepdims=True))
    centred = values - row_mean
    spread = lax.optimization_barrier(jnp.mean(centred * centred, -1, keepdims=True))
    return centred * lax.rsqrt(spread + eps)

def reference(candidates, in_weight, out_weight, page_cache, page_lists, hist_len):
    score_scale = 1.0 / math.sqrt(HD)
    positions = jnp.arange(MAXP * PAGE).astype(jnp.int32)

    def one_block(inputs):
        hidden_rows, block_lists, block_lengths = inputs
        divisors = (block_lengths + 1).astype(jnp.float32)
        cand_divisors = jnp.repeat(divisors, CPR)
        live_mask = positions[None, :] < block_lengths[:, None]
        flat_ids = block_lists.reshape(REQ_DEV * MAXP).astype(jnp.int32)
        for layer_index in range(LAYERS):
            normed = layer_norm(hidden_rows.astype(jnp.float32)).astype(jnp.bfloat16)
            projected = jnp.dot(normed, in_weight[layer_index].reshape(D, HEADS * 4 * HD), preferred_element_type=jnp.float32)
            projected = jax.nn.silu(projected).reshape(CAND_DEV, HEADS, 4 * HD)
            gate_part = projected[:, :, :HD]
            value_part = projected[:, :, HD:2 * HD].astype(jnp.bfloat16)
            query_part = projected[:, :, 2 * HD:3 * HD].astype(jnp.bfloat16)
            key_part = projected[:, :, 3 * HD:].astype(jnp.bfloat16)
            fetched = jnp.take(page_cache[layer_index], flat_ids, axis=0).reshape(REQ_DEV, MAXP, HEADS, 2, PAGE, HD)
            hist_keys = jnp.transpose(fetched[:, :, :, 0], (0, 2, 1, 3, 4)).reshape(REQ_DEV, HEADS, MAXP * PAGE, HD)
            hist_values = jnp.transpose(fetched[:, :, :, 1], (0, 2, 1, 3, 4)).reshape(REQ_DEV, HEADS, MAXP * PAGE, HD)
            queries = query_part.reshape(REQ_DEV, CPR, HEADS, HD)
            scores = jnp.einsum('rchd,rhtd->rhct', queries.astype(jnp.float32), hist_keys.astype(jnp.float32)) * score_scale
            weights = jnp.where(live_mask[:, None, None, :], jax.nn.silu(scores), 0.0) / divisors[:, None, None, None]
            weights = weights.astype(jnp.bfloat16)
            attended = jnp.einsum('rhct,rhtd->rchd', weights.astype(jnp.float32), hist_values.astype(jnp.float32))
            attended = attended.reshape(CAND_DEV, HEADS, HD)
            self_score = lax.optimization_barrier(jnp.sum(query_part.astype(jnp.float32) * key_part.astype(jnp.float32), -1)) * score_scale
            self_weight = (jax.nn.silu(self_score) / cand_divisors[:, None]).astype(jnp.bfloat16)
            attended = attended + self_weight.astype(jnp.float32)[:, :, None] * value_part.astype(jnp.float32)
            gated_rows = (layer_norm(attended) * gate_part).astype(jnp.bfloat16)
            head_terms = jnp.einsum('nhd,hde->nhe', gated_rows.astype(jnp.float32), out_weight[layer_index].astype(jnp.float32))
            group_terms = lax.optimization_barrier(jnp.sum(head_terms.reshape(CAND_DEV, N_HEADS, HEADS // N_HEADS, D), axis=2)).astype(jnp.bfloat16)
            hidden_rows = (hidden_rows.astype(jnp.float32) + lax.optimization_barrier(jnp.sum(group_terms.astype(jnp.float32), axis=1))).astype(jnp.bfloat16)
        return hidden_rows
    blocks = lax.map(one_block, (candidates.reshape(N_PAGES, CAND_DEV, D), page_lists.reshape(N_PAGES, REQ_DEV, MAXP), hist_len.reshape(N_PAGES, REQ_DEV)))
    return blocks.reshape(CANDS, D)
```

```python
import math

import jax
import jax.numpy as jnp
from jax import lax
from jax.sharding import PartitionSpec as P

eps = 1e-05


def layer_norm(values):
    row_mean = jnp.mean(values, -1, keepdims=True)
    centred = values - row_mean
    spread = jnp.mean(centred * centred, -1, keepdims=True)
    return centred * lax.rsqrt(spread + eps)


def gather_rows(rows):
    return lax.all_gather(rows, "heads", axis=0, tiled=True)


def scatter_sum(terms):
    return lax.psum_scatter(terms, "heads", scatter_dimension=0, tiled=True).astype(jnp.float32)


def on_device(candidates, in_weight, out_weight, page_cache, page_lists, hist_len):
    readers = lax.axis_size("pages")
    head_group = lax.axis_size("heads")
    layers = in_weight.shape[0]
    model_width = in_weight.shape[1]
    head_dim = out_weight.shape[2]
    pages_here = page_cache.shape[1]
    page_len = page_cache.shape[4]
    requests, max_pages = page_lists.shape
    slot_count = requests * max_pages
    capacity = 2 * slot_count // readers
    cand_rows = candidates.shape[0] * head_group
    per_request = cand_rows // requests
    history = max_pages * page_len
    score_scale = 1.0 / math.sqrt(head_dim)

    flat_ids = page_lists.reshape(slot_count)
    slot_owner = flat_ids // pages_here
    local_ids = flat_ids % pages_here
    slot_order = jnp.arange(slot_count)
    earlier_same = (slot_owner[None, :] == slot_owner[:, None]) & (
        slot_order[None, :] < slot_order[:, None]
    )
    slot_rank = jnp.sum(earlier_same.astype(jnp.int32), axis=1)
    places = slot_owner * capacity + slot_rank
    matches = places[None, :] == jnp.arange(readers * capacity)[:, None]
    asked = jnp.sum(jnp.where(matches, local_ids[None, :], 0), axis=1)
    wanted = lax.all_to_all(
        asked.reshape(readers, capacity), "pages", split_axis=0, concat_axis=0, tiled=True
    ).reshape(readers * capacity)

    histories = []
    for layer_index in range(layers):
        sent = jnp.take(page_cache[layer_index, :, 0], wanted, axis=0)
        if histories:
            sent, histories[-1] = lax.optimization_barrier((sent, histories[-1]))
        histories.append(
            lax.all_to_all(
                sent.reshape((readers, capacity) + sent.shape[1:]),
                "pages",
                split_axis=0,
                concat_axis=0,
                tiled=True,
            )
        )

    divisors = (hist_len + 1).astype(jnp.float32)
    cand_divisors = jnp.repeat(divisors, per_request)
    live = jnp.arange(history)[None, :] < hist_len[:, None]
    hidden_rows = candidates
    for layer_index in range(layers):
        weights_in = in_weight[layer_index].reshape(model_width, 4 * head_dim)
        ready = layer_norm(gather_rows(hidden_rows).astype(jnp.float32)).astype(jnp.bfloat16)
        projected = jax.nn.silu(jnp.dot(ready, weights_in, preferred_element_type=jnp.float32))
        gate_part = projected[:, :head_dim]
        value_part = projected[:, head_dim : 2 * head_dim].astype(jnp.bfloat16)
        query_part = projected[:, 2 * head_dim : 3 * head_dim].astype(jnp.bfloat16)
        key_part = projected[:, 3 * head_dim :].astype(jnp.bfloat16)
        got, query_part = lax.optimization_barrier((histories[layer_index], query_part))
        got = got.reshape(readers * capacity, 2, page_len, head_dim)
        listed = jnp.take(got, places, axis=0).reshape(requests, max_pages, 2, page_len, head_dim)
        hist_keys = listed[:, :, 0].reshape(requests, history, head_dim)
        hist_values = listed[:, :, 1].reshape(requests, history, head_dim)
        queries = query_part.reshape(requests, per_request, head_dim)
        scores = (
            jnp.einsum("rqd,rtd->rqt", queries, hist_keys, preferred_element_type=jnp.float32)
            * score_scale
        )
        weights = (
            jnp.where(live[:, None, :], jax.nn.silu(scores), 0.0) / divisors[:, None, None]
        ).astype(jnp.bfloat16)
        attended = jnp.einsum(
            "rqt,rtd->rqd", weights, hist_values, preferred_element_type=jnp.float32
        ).reshape(cand_rows, head_dim)
        self_score = (
            jnp.sum(query_part.astype(jnp.float32) * key_part.astype(jnp.float32), -1) * score_scale
        )
        self_weight = (jax.nn.silu(self_score) / cand_divisors).astype(jnp.bfloat16)
        attended = attended + self_weight.astype(jnp.float32)[:, None] * value_part.astype(
            jnp.float32
        )
        gated_rows = (layer_norm(attended) * gate_part).astype(jnp.bfloat16)
        weights_out = out_weight[layer_index].reshape(head_dim, model_width)
        terms = jnp.dot(gated_rows, weights_out, preferred_element_type=jnp.float32)
        summed = scatter_sum(terms.astype(jnp.bfloat16))
        hidden_rows = (hidden_rows.astype(jnp.float32) + summed).astype(jnp.bfloat16)
    return hidden_rows


def solution(mesh):
    in_specs = (
        P(("pages", "heads"), None),
        P(None, None, "heads", None),
        P(None, "heads", None, None),
        P(None, "pages", "heads", None, None, None),
        P("pages", None),
        P("pages"),
    )
    out_specs = P(("pages", "heads"), None)
    return jax.shard_map(
        on_device, mesh=mesh, in_specs=in_specs, out_specs=out_specs, check_vma=False
    )
```

```python
import functools
import math

import jax
import jax.numpy as jnp
from jax import lax
from jax.experimental import pallas as pl
from jax.experimental.pallas import tpu as pltpu
from jax.sharding import PartitionSpec as P

eps = 1e-05


def layer_norm(values):
    row_mean = jnp.mean(values, -1, keepdims=True)
    centred = values - row_mean
    spread = jnp.mean(centred * centred, -1, keepdims=True)
    return centred * lax.rsqrt(spread + eps)


X_SIZE = 4
Z_LO = 4
Z_SIZE = 8
CORES = 2
STRIDE = 2


def heads_index(x_pos, z_hi):
    return lax.rem(x_pos + X_SIZE, X_SIZE) * 2 + z_hi


def neighbours():
    page, head = lax.axis_index("pages"), lax.axis_index("heads")
    x_pos, z_hi = head // 2, lax.rem(head, 2)
    column = page // (Z_LO * CORES)
    z_lo, core = lax.rem(page // CORES, Z_LO), lax.rem(page, CORES)

    def at_z(step):
        z_pos = lax.rem(z_hi * Z_LO + z_lo + step + Z_SIZE, Z_SIZE)
        return ((column * Z_LO + lax.rem(z_pos, Z_LO)) * CORES + core, x_pos * 2 + z_pos // Z_LO)

    return dict(
        x=x_pos,
        z=z_hi,
        right=(page, heads_index(x_pos + 1, z_hi)),
        left=(page, heads_index(x_pos - 1, z_hi)),
        up=at_z(STRIDE),
        down=at_z(-STRIDE),
    )


def greet(near):
    barrier = pltpu.get_barrier_semaphore()
    partners = [near[side] for side in ("right", "left", "up", "down")]
    for partner in partners:
        pl.semaphore_signal(
            barrier, inc=1, device_id=partner, device_id_type=pl.DeviceIdType.MESH
        )
    pl.semaphore_wait(barrier, len(partners))


def remote(source, target, sems, place, device):
    return pltpu.make_async_remote_copy(
        src_ref=source,
        dst_ref=target,
        send_sem=sems.at[(0,) + place],
        recv_sem=sems.at[(1,) + place],
        device_id=device,
        device_id_type=pl.DeviceIdType.MESH,
    )


def wide(ref_block):
    return ref_block.astype(jnp.float32)


def z_relay(near, relay, z_sems, goal):
    started = []
    for half, (ahead, behind) in enumerate((("up", "down"), ("down", "up"))):
        remote(relay.at[half], relay.at[half], z_sems, (0, half), near[behind]).wait_recv()
        leg = remote(relay.at[half], goal(near[ahead], half), z_sems, (1, half), near[ahead])
        leg.start()
        started.append(leg)
    return started


def gather_phase(near, own, out, relay, z_sems, x_sems, f_sems):
    x_pos, z_hi = near["x"], near["z"]
    mine = heads_index(x_pos, z_hi)
    started = []

    def send(copy):
        copy.start()
        started.append(copy)

    def spread(source, slot, level, half):
        for side, name in (((0, "right"), (1, "left")) if half == 0 else ((1, "left"), (0, "right"))):
            send(remote(source, out.at[slot, half], x_sems, (side, level, half), near[name]))

    def pass_on(level, z_of):
        for side, (ahead, step) in enumerate((("right", -1), ("left", 1))):
            block = out.at[heads_index(x_pos + step, z_of), side]
            remote(block, block, x_sems, (side, level, side), near[ahead]).wait_recv()
            send(remote(block, block, f_sems, (side, level), near[ahead]))

    for half, ahead in enumerate(("up", "down")):
        send(remote(own.at[half], relay.at[half], z_sems, (0, half), near[ahead]))
    for half in range(2):
        spread(own.at[half], mine, 0, half)
    out[mine] = own[...]
    pass_on(0, z_hi)

    def goal(device, half):
        return out.at[heads_index(x_pos, 1 - lax.rem(device[1], 2)), half]

    started += z_relay(near, relay, z_sems, goal)
    theirs = heads_index(x_pos, 1 - z_hi)
    for half, behind in enumerate(("down", "up")):
        block = out.at[theirs, half]
        remote(block, block, z_sems, (1, half), near[behind]).wait_recv()
        spread(block, theirs, 1, half)
    pass_on(1, 1 - z_hi)
    for level, z_of in ((0, z_hi), (1, 1 - z_hi)):
        for side, (ahead, step) in enumerate((("right", -1), ("left", 1))):
            block = out.at[heads_index(x_pos + step, z_of), 1 - side]
            remote(block, block, x_sems, (side, level, 1 - side), near[ahead]).wait_recv()
            block = out.at[heads_index(x_pos + 2, z_of), side]
            remote(block, block, f_sems, (side, level), near[ahead]).wait_recv()
    for copy in started:
        copy.wait_send()


def reduce_phase(near, terms, first, direct, joined, joined_in, z_out, relay, z_in, z_sems, x_sems):
    x_pos, z_hi = near["x"], near["z"]
    z_of = (1 - z_hi, z_hi)
    ways = ("right", "left")
    steps = (1, -1)
    started = []

    def send(copy):
        copy.start()
        started.append(copy)

    def far(level):
        for side in range(2):
            block = terms.at[heads_index(x_pos + 2, z_of[level]), side]
            send(remote(block, first.at[level, side], x_sems, (0, level, side), near[ways[side]]))

    def near_by(level):
        for side in range(2):
            block = terms.at[heads_index(x_pos + steps[side], z_of[level]), 1 - side]
            send(remote(block, direct.at[level, side], x_sems, (1, level, side), near[ways[side]]))

    def join(level):
        for side in range(2):
            here = first.at[level, side]
            remote(here, here, x_sems, (0, level, side), near[ways[side]]).wait_recv()
            own = terms[heads_index(x_pos + steps[side], z_of[level]), side]
            joined[level, side] = (wide(own) + wide(here[...])).astype(jnp.bfloat16)
            send(
                remote(
                    joined.at[level, side],
                    joined_in.at[level, side],
                    x_sems,
                    (2, level, side),
                    near[ways[side]],
                )
            )

    def total(level, half):
        here = joined_in.at[level, half]
        remote(here, here, x_sems, (2, level, half), near[ways[half]]).wait_recv()
        other = direct.at[level, 1 - half]
        remote(other, other, x_sems, (1, level, 1 - half), near[ways[1 - half]]).wait_recv()
        own = terms[heads_index(x_pos, z_of[level]), half]
        return wide(own) + wide(here[...]) + wide(other[...])

    far(0)
    near_by(0)
    far(1)
    join(0)
    near_by(1)
    join(1)
    for half, ahead in enumerate(("up", "down")):
        z_out[half] = total(0, half).astype(jnp.bfloat16)
        send(remote(z_out.at[half], relay.at[half], z_sems, (0, half), near[ahead]))
    sums = [total(1, half) for half in range(2)]
    started += z_relay(near, relay, z_sems, lambda device, half: z_in.at[half])
    for half, behind in enumerate(("down", "up")):
        here = z_in.at[half]
        remote(here, here, z_sems, (1, half), near[behind]).wait_recv()
        sums[half] = sums[half] + wide(here[...])
    for copy in started:
        copy.wait_send()
    return sums


def gather_kernel(own, out, *scratch):
    near = neighbours()
    greet(near)
    gather_phase(near, own, out, *scratch)


def reduce_kernel(terms, hidden, new_hidden, *scratch):
    near = neighbours()
    greet(near)
    sums = reduce_phase(near, terms, *scratch)
    for half in range(2):
        new_hidden[half] = (wide(hidden[half]) + sums[half]).astype(jnp.bfloat16)


def reduce_gather_kernel(split, terms, hidden, new_hidden, out, own, *scratch):
    near = neighbours()
    greet(near)
    sums = reduce_phase(near, terms, *scratch[:split])
    for half in range(2):
        rounded = (wide(hidden[half]) + sums[half]).astype(jnp.bfloat16)
        new_hidden[half] = rounded
        own[half] = layer_norm(wide(rounded)).astype(jnp.bfloat16)
    gather_phase(near, own, out, *scratch[split:])


def exchange(hidden, terms, gather, collective_id):
    rows, width = hidden.shape
    group = lax.axis_size("heads")
    half_rows = rows // 2
    halves = (half_rows, width)
    block = pltpu.VMEM((2,) + halves, jnp.bfloat16)
    pair = pltpu.VMEM((2, 2) + halves, jnp.bfloat16)
    gathering = [
        block,
        pltpu.SemaphoreType.DMA((2, 2, 2)),
        pltpu.SemaphoreType.DMA((2, 2, 2, 2)),
        pltpu.SemaphoreType.DMA((2, 2, 2)),
    ]
    reducing = [pair, pair, pair, pair, block, block, block]
    reducing += [pltpu.SemaphoreType.DMA((2, 2, 2)), pltpu.SemaphoreType.DMA((2, 3, 2, 2))]
    one = jax.ShapeDtypeStruct((2,) + halves, jnp.bfloat16)
    whole = jax.ShapeDtypeStruct((group, 2) + halves, jnp.bfloat16)
    if terms is None:
        kernel, shapes, scratch = gather_kernel, [whole], gathering
        given = [layer_norm(hidden.astype(jnp.float32)).astype(jnp.bfloat16).reshape(one.shape)]
    else:
        given = [terms.reshape(whole.shape), hidden.reshape(one.shape)]
        if gather:
            kernel = functools.partial(reduce_gather_kernel, len(reducing))
            shapes, scratch = [one, whole], [block] + reducing + gathering
        else:
            kernel, shapes, scratch = reduce_kernel, [one], reducing
    in_vmem = pl.BlockSpec(memory_space=pltpu.VMEM)
    results = pl.pallas_call(
        kernel,
        out_shape=shapes,
        in_specs=[in_vmem] * len(given),
        out_specs=[in_vmem] * len(shapes),
        scratch_shapes=scratch,
        compiler_params=pltpu.CompilerParams(collective_id=collective_id, has_side_effects=True),
    )(*given)
    new_hidden = hidden if terms is None else results[0].reshape(rows, width)
    ready = results[-1].reshape(group * rows, width) if gather else None
    return new_hidden, ready


def on_device(candidates, in_weight, out_weight, page_cache, page_lists, hist_len):
    readers = lax.axis_size("pages")
    head_group = lax.axis_size("heads")
    layers = in_weight.shape[0]
    model_width = in_weight.shape[1]
    head_dim = out_weight.shape[2]
    pages_here = page_cache.shape[1]
    page_len = page_cache.shape[4]
    requests, max_pages = page_lists.shape
    slot_count = requests * max_pages
    capacity = 2 * slot_count // readers
    cand_rows = candidates.shape[0] * head_group
    per_request = cand_rows // requests
    history = max_pages * page_len
    score_scale = 1.0 / math.sqrt(head_dim)

    flat_ids = page_lists.reshape(slot_count)
    slot_owner = flat_ids // pages_here
    local_ids = flat_ids % pages_here
    slot_order = jnp.arange(slot_count)
    earlier_same = (slot_owner[None, :] == slot_owner[:, None]) & (
        slot_order[None, :] < slot_order[:, None]
    )
    slot_rank = jnp.sum(earlier_same.astype(jnp.int32), axis=1)
    places = slot_owner * capacity + slot_rank
    matches = places[None, :] == jnp.arange(readers * capacity)[:, None]
    asked = jnp.sum(jnp.where(matches, local_ids[None, :], 0), axis=1)
    wanted = lax.all_to_all(
        asked.reshape(readers, capacity), "pages", split_axis=0, concat_axis=0, tiled=True
    ).reshape(readers * capacity)

    histories = []
    for layer_index in range(layers):
        sent = jnp.take(page_cache[layer_index, :, 0], wanted, axis=0)
        if histories:
            sent, histories[-1] = lax.optimization_barrier((sent, histories[-1]))
        histories.append(
            lax.all_to_all(
                sent.reshape((readers, capacity) + sent.shape[1:]),
                "pages",
                split_axis=0,
                concat_axis=0,
                tiled=True,
            )
        )

    divisors = (hist_len + 1).astype(jnp.float32)
    cand_divisors = jnp.repeat(divisors, per_request)
    live = jnp.arange(history)[None, :] < hist_len[:, None]
    hidden_rows, ready = exchange(candidates, None, True, 0)
    for layer_index in range(layers):
        weights_in = in_weight[layer_index].reshape(model_width, 4 * head_dim)
        projected = jax.nn.silu(jnp.dot(ready, weights_in, preferred_element_type=jnp.float32))
        gate_part = projected[:, :head_dim]
        value_part = projected[:, head_dim : 2 * head_dim].astype(jnp.bfloat16)
        query_part = projected[:, 2 * head_dim : 3 * head_dim].astype(jnp.bfloat16)
        key_part = projected[:, 3 * head_dim :].astype(jnp.bfloat16)
        got, query_part = lax.optimization_barrier((histories[layer_index], query_part))
        got = got.reshape(readers * capacity, 2, page_len, head_dim)
        listed = jnp.take(got, places, axis=0).reshape(requests, max_pages, 2, page_len, head_dim)
        hist_keys = listed[:, :, 0].reshape(requests, history, head_dim)
        hist_values = listed[:, :, 1].reshape(requests, history, head_dim)
        queries = query_part.reshape(requests, per_request, head_dim)
        scores = (
            jnp.einsum("rqd,rtd->rqt", queries, hist_keys, preferred_element_type=jnp.float32)
            * score_scale
        )
        weights = (
            jnp.where(live[:, None, :], jax.nn.silu(scores), 0.0) / divisors[:, None, None]
        ).astype(jnp.bfloat16)
        attended = jnp.einsum(
            "rqt,rtd->rqd", weights, hist_values, preferred_element_type=jnp.float32
        ).reshape(cand_rows, head_dim)
        self_score = (
            jnp.sum(query_part.astype(jnp.float32) * key_part.astype(jnp.float32), -1) * score_scale
        )
        self_weight = (jax.nn.silu(self_score) / cand_divisors).astype(jnp.bfloat16)
        attended = attended + self_weight.astype(jnp.float32)[:, None] * value_part.astype(
            jnp.float32
        )
        gated_rows = (layer_norm(attended) * gate_part).astype(jnp.bfloat16)
        weights_out = out_weight[layer_index].reshape(head_dim, model_width)
        terms = jnp.dot(gated_rows, weights_out, preferred_element_type=jnp.float32)
        hidden_rows, ready = exchange(
            hidden_rows, terms.astype(jnp.bfloat16), layer_index + 1 < layers, layer_index + 1
        )
    return hidden_rows


def solution(mesh):
    in_specs = (
        P(("pages", "heads"), None),
        P(None, None, "heads", None),
        P(None, "heads", None, None),
        P(None, "pages", "heads", None, None, None),
        P("pages", None),
        P("pages"),
    )
    out_specs = P(("pages", "heads"), None)
    return jax.shard_map(
        on_device, mesh=mesh, in_specs=in_specs, out_specs=out_specs, check_vma=False
    )
```

```python
import functools
import math

import jax
import jax.numpy as jnp
from jax import lax
from jax.experimental import pallas as pl
from jax.experimental.pallas import tpu as pltpu
from jax.sharding import PartitionSpec as P

eps = 1e-05


def layer_norm(values):
    row_mean = jnp.mean(values, -1, keepdims=True)
    centred = values - row_mean
    spread = jnp.mean(centred * centred, -1, keepdims=True)
    return centred * lax.rsqrt(spread + eps)


X_SIZE = 4
Z_LO = 4
Z_SIZE = 8
CORES = 2
STRIDE = 2


def heads_index(x_pos, z_hi):
    return lax.rem(x_pos + X_SIZE, X_SIZE) * 2 + z_hi


def neighbours():
    page, head = lax.axis_index("pages"), lax.axis_index("heads")
    x_pos, z_hi = head // 2, lax.rem(head, 2)
    column = page // (Z_LO * CORES)
    z_lo, core = lax.rem(page // CORES, Z_LO), lax.rem(page, CORES)

    def at_z(step):
        z_pos = lax.rem(z_hi * Z_LO + z_lo + step + Z_SIZE, Z_SIZE)
        return ((column * Z_LO + lax.rem(z_pos, Z_LO)) * CORES + core, x_pos * 2 + z_pos // Z_LO)

    return dict(
        x=x_pos,
        z=z_hi,
        right=(page, heads_index(x_pos + 1, z_hi)),
        left=(page, heads_index(x_pos - 1, z_hi)),
        up=at_z(STRIDE),
        down=at_z(-STRIDE),
    )


def greet(near):
    barrier = pltpu.get_barrier_semaphore()
    partners = [near[side] for side in ("right", "left", "up", "down")]
    for partner in partners:
        pl.semaphore_signal(
            barrier, inc=1, device_id=partner, device_id_type=pl.DeviceIdType.MESH
        )
    pl.semaphore_wait(barrier, len(partners))


def remote(source, target, sems, place, device):
    return pltpu.make_async_remote_copy(
        src_ref=source,
        dst_ref=target,
        send_sem=sems.at[(0,) + place],
        recv_sem=sems.at[(1,) + place],
        device_id=device,
        device_id_type=pl.DeviceIdType.MESH,
    )


def wide(ref_block):
    return ref_block.astype(jnp.float32)


def z_relay(near, relay, z_sems, goal):
    started = []
    for half, (ahead, behind) in enumerate((("up", "down"), ("down", "up"))):
        remote(relay.at[half], relay.at[half], z_sems, (0, half), near[behind]).wait_recv()
        leg = remote(relay.at[half], goal(near[ahead], half), z_sems, (1, half), near[ahead])
        leg.start()
        started.append(leg)
    return started


def gather_phase(near, own, out, relay, z_sems, x_sems, f_sems):
    x_pos, z_hi = near["x"], near["z"]
    mine = heads_index(x_pos, z_hi)
    started = []

    def send(copy):
        copy.start()
        started.append(copy)

    def spread(source, slot, level, half):
        for side, name in (((0, "right"), (1, "left")) if half == 0 else ((1, "left"), (0, "right"))):
            send(remote(source, out.at[slot, half], x_sems, (side, level, half), near[name]))

    def pass_on(level, z_of):
        for side, (ahead, step) in enumerate((("right", -1), ("left", 1))):
            block = out.at[heads_index(x_pos + step, z_of), side]
            remote(block, block, x_sems, (side, level, side), near[ahead]).wait_recv()
            send(remote(block, block, f_sems, (side, level), near[ahead]))

    for half, ahead in enumerate(("up", "down")):
        send(remote(own.at[half], relay.at[half], z_sems, (0, half), near[ahead]))
    for half in range(2):
        spread(own.at[half], mine, 0, half)
    out[mine] = own[...]
    pass_on(0, z_hi)

    def goal(device, half):
        return out.at[heads_index(x_pos, 1 - lax.rem(device[1], 2)), half]

    started += z_relay(near, relay, z_sems, goal)
    theirs = heads_index(x_pos, 1 - z_hi)
    for half, behind in enumerate(("down", "up")):
        block = out.at[theirs, half]
        remote(block, block, z_sems, (1, half), near[behind]).wait_recv()
        spread(block, theirs, 1, half)
    pass_on(1, 1 - z_hi)
    for level, z_of in ((0, z_hi), (1, 1 - z_hi)):
        for side, (ahead, step) in enumerate((("right", -1), ("left", 1))):
            block = out.at[heads_index(x_pos + step, z_of), 1 - side]
            remote(block, block, x_sems, (side, level, 1 - side), near[ahead]).wait_recv()
            block = out.at[heads_index(x_pos + 2, z_of), side]
            remote(block, block, f_sems, (side, level), near[ahead]).wait_recv()
    for copy in started:
        copy.wait_send()


def reduce_phase(near, terms, first, direct, joined, joined_in, z_out, relay, z_in, z_sems, x_sems):
    x_pos, z_hi = near["x"], near["z"]
    z_of = (1 - z_hi, z_hi)
    ways = ("right", "left")
    steps = (1, -1)
    started = []

    def send(copy):
        copy.start()
        started.append(copy)

    def far(level):
        for side in range(2):
            block = terms.at[heads_index(x_pos + 2, z_of[level]), side]
            send(remote(block, first.at[level, side], x_sems, (0, level, side), near[ways[side]]))

    def near_by(level):
        for side in range(2):
            block = terms.at[heads_index(x_pos + steps[side], z_of[level]), 1 - side]
            send(remote(block, direct.at[level, side], x_sems, (1, level, side), near[ways[side]]))

    def join(level):
        for side in range(2):
            here = first.at[level, side]
            remote(here, here, x_sems, (0, level, side), near[ways[side]]).wait_recv()
            own = terms[heads_index(x_pos + steps[side], z_of[level]), side]
            joined[level, side] = (wide(own) + wide(here[...])).astype(jnp.bfloat16)
            send(
                remote(
                    joined.at[level, side],
                    joined_in.at[level, side],
                    x_sems,
                    (2, level, side),
                    near[ways[side]],
                )
            )

    def total(level, half):
        here = joined_in.at[level, half]
        remote(here, here, x_sems, (2, level, half), near[ways[half]]).wait_recv()
        other = direct.at[level, 1 - half]
        remote(other, other, x_sems, (1, level, 1 - half), near[ways[1 - half]]).wait_recv()
        own = terms[heads_index(x_pos, z_of[level]), half]
        return wide(own) + wide(here[...]) + wide(other[...])

    far(0)
    near_by(0)
    far(1)
    join(0)
    near_by(1)
    join(1)
    for half, ahead in enumerate(("up", "down")):
        z_out[half] = total(0, half).astype(jnp.bfloat16)
        send(remote(z_out.at[half], relay.at[half], z_sems, (0, half), near[ahead]))
    sums = [total(1, half) for half in range(2)]
    started += z_relay(near, relay, z_sems, lambda device, half: z_in.at[half])
    for half, behind in enumerate(("down", "up")):
        here = z_in.at[half]
        remote(here, here, z_sems, (1, half), near[behind]).wait_recv()
        sums[half] = sums[half] + wide(here[...])
    for copy in started:
        copy.wait_send()
    return sums


def gather_kernel(own, out, *scratch):
    near = neighbours()
    greet(near)
    gather_phase(near, own, out, *scratch)


def reduce_kernel(terms, hidden, new_hidden, *scratch):
    near = neighbours()
    greet(near)
    sums = reduce_phase(near, terms, *scratch)
    for half in range(2):
        new_hidden[half] = (wide(hidden[half]) + sums[half]).astype(jnp.bfloat16)


def reduce_gather_kernel(split, terms, hidden, new_hidden, out, own, *scratch):
    near = neighbours()
    greet(near)
    sums = reduce_phase(near, terms, *scratch[:split])
    for half in range(2):
        rounded = (wide(hidden[half]) + sums[half]).astype(jnp.bfloat16)
        new_hidden[half] = rounded
        own[half] = layer_norm(wide(rounded)).astype(jnp.bfloat16)
    gather_phase(near, own, out, *scratch[split:])


def exchange(hidden, terms, gather, collective_id):
    rows, width = hidden.shape
    group = lax.axis_size("heads")
    half_rows = rows // 2
    halves = (half_rows, width)
    block = pltpu.VMEM((2,) + halves, jnp.bfloat16)
    pair = pltpu.VMEM((2, 2) + halves, jnp.bfloat16)
    gathering = [
        block,
        pltpu.SemaphoreType.DMA((2, 2, 2)),
        pltpu.SemaphoreType.DMA((2, 2, 2, 2)),
        pltpu.SemaphoreType.DMA((2, 2, 2)),
    ]
    reducing = [pair, pair, pair, pair, block, block, block]
    reducing += [pltpu.SemaphoreType.DMA((2, 2, 2)), pltpu.SemaphoreType.DMA((2, 3, 2, 2))]
    one = jax.ShapeDtypeStruct((2,) + halves, jnp.bfloat16)
    whole = jax.ShapeDtypeStruct((group, 2) + halves, jnp.bfloat16)
    if terms is None:
        kernel, shapes, scratch = gather_kernel, [whole], gathering
        given = [layer_norm(hidden.astype(jnp.float32)).astype(jnp.bfloat16).reshape(one.shape)]
    else:
        given = [terms.reshape(whole.shape), hidden.reshape(one.shape)]
        if gather:
            kernel = functools.partial(reduce_gather_kernel, len(reducing))
            shapes, scratch = [one, whole], [block] + reducing + gathering
        else:
            kernel, shapes, scratch = reduce_kernel, [one], reducing
    in_vmem = pl.BlockSpec(memory_space=pltpu.VMEM)
    results = pl.pallas_call(
        kernel,
        out_shape=shapes,
        in_specs=[in_vmem] * len(given),
        out_specs=[in_vmem] * len(shapes),
        scratch_shapes=scratch,
        compiler_params=pltpu.CompilerParams(collective_id=collective_id, has_side_effects=True),
    )(*given)
    new_hidden = hidden if terms is None else results[0].reshape(rows, width)
    ready = results[-1].reshape(group * rows, width) if gather else None
    return new_hidden, ready


def on_device(candidates, in_weight, out_weight, page_cache, page_lists, hist_len):
    readers = lax.axis_size("pages")
    head_group = lax.axis_size("heads")
    layers = in_weight.shape[0]
    model_width = in_weight.shape[1]
    head_dim = out_weight.shape[2]
    pages_here = page_cache.shape[1]
    page_len = page_cache.shape[4]
    requests, max_pages = page_lists.shape
    slot_count = requests * max_pages
    capacity = 2 * slot_count // readers
    cand_rows = candidates.shape[0] * head_group
    per_request = cand_rows // requests
    history = max_pages * page_len
    score_scale = 1.0 / math.sqrt(head_dim)

    flat_ids = page_lists.reshape(slot_count)
    slot_owner = flat_ids // pages_here
    local_ids = flat_ids % pages_here
    slot_order = jnp.arange(slot_count)
    earlier_same = (slot_owner[None, :] == slot_owner[:, None]) & (
        slot_order[None, :] < slot_order[:, None]
    )
    slot_rank = jnp.sum(earlier_same.astype(jnp.int32), axis=1)
    places = slot_owner * capacity + slot_rank
    matches = places[None, :] == jnp.arange(readers * capacity)[:, None]
    asked = jnp.sum(jnp.where(matches, local_ids[None, :], 0), axis=1)
    wanted = lax.all_to_all(
        asked.reshape(readers, capacity), "pages", split_axis=0, concat_axis=0, tiled=True
    ).reshape(readers * capacity)

    def history_of(layer_index, after):
        rows = page_cache.at[layer_index, wanted, 0].get(mode="promise_in_bounds")
        rows, after = lax.optimization_barrier((rows, after))
        rows = rows.reshape((readers, capacity) + rows.shape[1:])
        return lax.all_to_all(rows, "pages", split_axis=0, concat_axis=0, tiled=True), after

    hidden_rows, ready = exchange(candidates, None, True, 0)
    history_now, ready = history_of(0, ready)
    divisors = (hist_len + 1).astype(jnp.float32)
    cand_divisors = jnp.repeat(divisors, per_request)
    live = jnp.arange(history)[None, :] < hist_len[:, None]
    for layer_index in range(layers):
        weights_in = in_weight[layer_index].reshape(model_width, 4 * head_dim)
        projected = jax.nn.silu(jnp.dot(ready, weights_in, preferred_element_type=jnp.float32))
        gate_part = projected[:, :head_dim]
        value_part = projected[:, head_dim : 2 * head_dim].astype(jnp.bfloat16)
        query_part = projected[:, 2 * head_dim : 3 * head_dim].astype(jnp.bfloat16)
        key_part = projected[:, 3 * head_dim :].astype(jnp.bfloat16)
        if layer_index + 1 < layers:
            history_next, query_part = history_of(layer_index + 1, query_part)
        got, query_part = lax.optimization_barrier((history_now, query_part))
        got = got.reshape(readers * capacity, 2, page_len, head_dim)
        listed = got.at[places].get(mode="promise_in_bounds").reshape(requests, max_pages, 2, page_len, head_dim)
        hist_keys = listed[:, :, 0].reshape(requests, history, head_dim)
        hist_values = listed[:, :, 1].reshape(requests, history, head_dim)
        queries = query_part.reshape(requests, per_request, head_dim)
        scores = (
            jnp.einsum("rqd,rtd->rqt", queries, hist_keys, preferred_element_type=jnp.float32)
            * score_scale
        )
        weights = (
            jnp.where(live[:, None, :], jax.nn.silu(scores), 0.0) / divisors[:, None, None]
        ).astype(jnp.bfloat16)
        attended = jnp.einsum(
            "rqt,rtd->rqd", weights, hist_values, preferred_element_type=jnp.float32
        ).reshape(cand_rows, head_dim)
        self_score = (
            jnp.sum(query_part.astype(jnp.float32) * key_part.astype(jnp.float32), -1) * score_scale
        )
        self_weight = (jax.nn.silu(self_score) / cand_divisors).astype(jnp.bfloat16)
        attended = attended + self_weight.astype(jnp.float32)[:, None] * value_part.astype(
            jnp.float32
        )
        gated_rows = (layer_norm(attended) * gate_part).astype(jnp.bfloat16)
        weights_out = out_weight[layer_index].reshape(head_dim, model_width)
        terms = jnp.dot(gated_rows, weights_out, preferred_element_type=jnp.float32)
        hidden_rows, ready = exchange(
            hidden_rows, terms.astype(jnp.bfloat16), layer_index + 1 < layers, layer_index + 1
        )
        history_now = history_next
    return hidden_rows


def solution(mesh):
    in_specs = (
        P(("pages", "heads"), None),
        P(None, None, "heads", None),
        P(None, "heads", None, None),
        P(None, "pages", "heads", None, None, None),
        P("pages", None),
        P("pages"),
    )
    out_specs = P(("pages", "heads"), None)
    return jax.shard_map(
        on_device, mesh=mesh, in_specs=in_specs, out_specs=out_specs, check_vma=False
    )
```

```python
import math

import jax
import jax.numpy as jnp
from jax import lax
from jax.experimental import pallas as pl
from jax.experimental.pallas import tpu as pltpu
from jax.sharding import PartitionSpec as P

eps = 1e-05


def layer_norm(values):
    row_mean = jnp.mean(values, -1, keepdims=True)
    centred = values - row_mean
    spread = jnp.mean(centred * centred, -1, keepdims=True)
    return centred * lax.rsqrt(spread + eps)


X_SIZE = 4
Z_LO = 4
Z_SIZE = 8
CORES = 2
STRIDE = 2


def heads_index(x_pos, z_hi):
    return lax.rem(x_pos + X_SIZE, X_SIZE) * 2 + z_hi


def neighbours():
    page, head = lax.axis_index("pages"), lax.axis_index("heads")
    x_pos, z_hi = head // 2, lax.rem(head, 2)
    column = page // (Z_LO * CORES)
    z_lo, core = lax.rem(page // CORES, Z_LO), lax.rem(page, CORES)

    def at_z(step):
        z_pos = lax.rem(z_hi * Z_LO + z_lo + step + Z_SIZE, Z_SIZE)
        return ((column * Z_LO + lax.rem(z_pos, Z_LO)) * CORES + core, x_pos * 2 + z_pos // Z_LO)

    return dict(
        x=x_pos,
        z=z_hi,
        right=(page, heads_index(x_pos + 1, z_hi)),
        left=(page, heads_index(x_pos - 1, z_hi)),
        up=at_z(STRIDE),
        down=at_z(-STRIDE),
    )


def greet(near):
    barrier = pltpu.get_barrier_semaphore()
    partners = [near[side] for side in ("right", "left", "up", "down")]
    for partner in partners:
        pl.semaphore_signal(
            barrier, inc=1, device_id=partner, device_id_type=pl.DeviceIdType.MESH
        )
    pl.semaphore_wait(barrier, len(partners))


def remote(source, target, sems, place, device):
    return pltpu.make_async_remote_copy(
        src_ref=source,
        dst_ref=target,
        send_sem=sems.at[(0,) + place],
        recv_sem=sems.at[(1,) + place],
        device_id=device,
        device_id_type=pl.DeviceIdType.MESH,
    )


def wide(ref_block):
    return ref_block.astype(jnp.float32)


def z_relay(near, relay, z_sems, goal):
    started = []
    for half, (ahead, behind) in enumerate((("up", "down"), ("down", "up"))):
        remote(relay.at[half], relay.at[half], z_sems, (0, half), near[behind]).wait_recv()
        leg = remote(relay.at[half], goal(near[ahead], half), z_sems, (1, half), near[ahead])
        leg.start()
        started.append(leg)
    return started


def gather_phase(near, own, out, relay, z_sems, x_sems, f_sems):
    x_pos, z_hi = near["x"], near["z"]
    mine = heads_index(x_pos, z_hi)
    started = []

    def send(copy):
        copy.start()
        started.append(copy)

    def spread(source, slot, level, half):
        for side, name in (((0, "right"), (1, "left")) if half == 0 else ((1, "left"), (0, "right"))):
            send(remote(source, out.at[slot, half], x_sems, (side, level, half), near[name]))

    def pass_on(level, z_of):
        for side, (ahead, step) in enumerate((("right", -1), ("left", 1))):
            block = out.at[heads_index(x_pos + step, z_of), side]
            remote(block, block, x_sems, (side, level, side), near[ahead]).wait_recv()
            send(remote(block, block, f_sems, (side, level), near[ahead]))

    for half, ahead in enumerate(("up", "down")):
        send(remote(own.at[half], relay.at[half], z_sems, (0, half), near[ahead]))
    for half in range(2):
        spread(own.at[half], mine, 0, half)
    out[mine] = own[...]
    pass_on(0, z_hi)

    def goal(device, half):
        return out.at[heads_index(x_pos, 1 - lax.rem(device[1], 2)), half]

    started += z_relay(near, relay, z_sems, goal)
    theirs = heads_index(x_pos, 1 - z_hi)
    for half, behind in enumerate(("down", "up")):
        block = out.at[theirs, half]
        remote(block, block, z_sems, (1, half), near[behind]).wait_recv()
        spread(block, theirs, 1, half)
    pass_on(1, 1 - z_hi)
    for level, z_of in ((0, z_hi), (1, 1 - z_hi)):
        for side, (ahead, step) in enumerate((("right", -1), ("left", 1))):
            block = out.at[heads_index(x_pos + step, z_of), 1 - side]
            remote(block, block, x_sems, (side, level, 1 - side), near[ahead]).wait_recv()
            block = out.at[heads_index(x_pos + 2, z_of), side]
            remote(block, block, f_sems, (side, level), near[ahead]).wait_recv()
    for copy in started:
        copy.wait_send()


def sum_along_x(near, terms, first, direct, joined, joined_in, x_sems):
    x_pos, z_hi = near["x"], near["z"]
    z_of = (1 - z_hi, z_hi)
    ways = ("right", "left")
    steps = (1, -1)
    started = []

    def send(copy):
        copy.start()
        started.append(copy)

    def far(level):
        for side in range(2):
            block = terms.at[heads_index(x_pos + 2, z_of[level]), side]
            send(remote(block, first.at[level, side], x_sems, (0, level, side), near[ways[side]]))

    def near_by(level):
        for side in range(2):
            block = terms.at[heads_index(x_pos + steps[side], z_of[level]), 1 - side]
            send(remote(block, direct.at[level, side], x_sems, (1, level, side), near[ways[side]]))

    def join(level):
        for side in range(2):
            here = first.at[level, side]
            remote(here, here, x_sems, (0, level, side), near[ways[side]]).wait_recv()
            own = terms[heads_index(x_pos + steps[side], z_of[level]), side]
            joined[level, side] = (wide(own) + wide(here[...])).astype(jnp.bfloat16)
            send(
                remote(
                    joined.at[level, side],
                    joined_in.at[level, side],
                    x_sems,
                    (2, level, side),
                    near[ways[side]],
                )
            )

    def total(level, half):
        here = joined_in.at[level, half]
        remote(here, here, x_sems, (2, level, half), near[ways[half]]).wait_recv()
        other = direct.at[level, 1 - half]
        remote(other, other, x_sems, (1, level, 1 - half), near[ways[1 - half]]).wait_recv()
        own = terms[heads_index(x_pos, z_of[level]), half]
        return wide(own) + wide(here[...]) + wide(other[...])

    far(0)
    near_by(0)
    far(1)
    join(0)
    near_by(1)
    join(1)
    return total, started


def reduce_phase(near, terms, first, direct, joined, joined_in, z_out, relay, z_in, z_sems, x_sems):
    total, started = sum_along_x(near, terms, first, direct, joined, joined_in, x_sems)

    def send(copy):
        copy.start()
        started.append(copy)

    for half, ahead in enumerate(("up", "down")):
        z_out[half] = total(0, half).astype(jnp.bfloat16)
        send(remote(z_out.at[half], relay.at[half], z_sems, (0, half), near[ahead]))
    sums = [total(1, half) for half in range(2)]
    started += z_relay(near, relay, z_sems, lambda device, half: z_in.at[half])
    for half, behind in enumerate(("down", "up")):
        here = z_in.at[half]
        remote(here, here, z_sems, (1, half), near[behind]).wait_recv()
        sums[half] = sums[half] + wide(here[...])
    for copy in started:
        copy.wait_send()
    return sums


def gather_kernel(own, out, *scratch):
    near = neighbours()
    greet(near)
    gather_phase(near, own, out, *scratch)


def reduce_kernel(terms, hidden, new_hidden, *scratch):
    near = neighbours()
    greet(near)
    sums = reduce_phase(near, terms, *scratch)
    for half in range(2):
        new_hidden[half] = (wide(hidden[half]) + sums[half]).astype(jnp.bfloat16)


def reduce_gather_kernel(
    terms, hidden, new_hidden, out, first, direct, joined, joined_in,
    z_out, relay, z_in, own, z_sems, x_sems, g_sems, f_sems
):
    near = neighbours()
    greet(near)
    x_pos, z_hi = near["x"], near["z"]
    z_of = (1 - z_hi, z_hi)
    ways = (("right", -1), ("left", 1))
    total, started = sum_along_x(near, terms, first, direct, joined, joined_in, x_sems)

    def send(copy):
        copy.start()
        started.append(copy)

    for level in range(2):
        for half, ahead in enumerate(("up", "down")):
            partial = total(level, half)
            if level == 1:
                partial = partial + wide(hidden[half])
            z_out[level, half] = partial.astype(jnp.bfloat16)
            place = relay.at[level, half]
            send(remote(z_out.at[level, half], place, z_sems, (0, level, half), near[ahead]))
    for level in range(2):
        for half, (ahead, behind) in enumerate((("up", "down"), ("down", "up"))):
            place = relay.at[level, half]
            remote(place, place, z_sems, (0, level, half), near[behind]).wait_recv()
            target = z_in.at[1 - level, half]
            send(remote(place, target, z_sems, (1, level, half), near[ahead]))
    for level in (1, 0):
        slot = heads_index(x_pos, z_of[level])
        for half, behind in enumerate(("down", "up")):
            here = z_in.at[level, half]
            remote(here, here, z_sems, (1, 1 - level, half), near[behind]).wait_recv()
            rounded = (wide(z_out[level, half]) + wide(here[...])).astype(jnp.bfloat16)
            if level == 1:
                new_hidden[half] = rounded
            own[level, half] = layer_norm(wide(rounded)).astype(jnp.bfloat16)
            for side in (half, 1 - half):
                target = out.at[slot, half]
                device = near[ways[side][0]]
                send(remote(own.at[level, half], target, g_sems, (side, level, half), device))
        out[slot] = own[level]
    for level in (1, 0):
        for side, (ahead, step) in enumerate(ways):
            block = out.at[heads_index(x_pos + step, z_of[level]), side]
            remote(block, block, g_sems, (side, level, side), near[ahead]).wait_recv()
            send(remote(block, block, f_sems, (side, level), near[ahead]))
    for level in (1, 0):
        for side, (ahead, step) in enumerate(ways):
            block = out.at[heads_index(x_pos + step, z_of[level]), 1 - side]
            remote(block, block, g_sems, (side, level, 1 - side), near[ahead]).wait_recv()
            block = out.at[heads_index(x_pos + 2, z_of[level]), side]
            remote(block, block, f_sems, (side, level), near[ahead]).wait_recv()
    for copy in started:
        copy.wait_send()


def exchange(hidden, terms, gather, collective_id):
    rows, width = hidden.shape
    group = lax.axis_size("heads")
    half_rows = rows // 2
    halves = (half_rows, width)
    block = pltpu.VMEM((2,) + halves, jnp.bfloat16)
    pair = pltpu.VMEM((2, 2) + halves, jnp.bfloat16)
    gathering = [
        block,
        pltpu.SemaphoreType.DMA((2, 2, 2)),
        pltpu.SemaphoreType.DMA((2, 2, 2, 2)),
        pltpu.SemaphoreType.DMA((2, 2, 2)),
    ]
    reducing = [pair, pair, pair, pair, block, block, block]
    reducing += [pltpu.SemaphoreType.DMA((2, 2, 2)), pltpu.SemaphoreType.DMA((2, 3, 2, 2))]
    one = jax.ShapeDtypeStruct((2,) + halves, jnp.bfloat16)
    whole = jax.ShapeDtypeStruct((group, 2) + halves, jnp.bfloat16)
    if terms is None:
        kernel, shapes, scratch = gather_kernel, [whole], gathering
        given = [layer_norm(hidden.astype(jnp.float32)).astype(jnp.bfloat16).reshape(one.shape)]
    else:
        given = [terms.reshape(whole.shape), hidden.reshape(one.shape)]
        if gather:
            kernel, shapes = reduce_gather_kernel, [one, whole]
            scratch = [pair] * 8 + [pltpu.SemaphoreType.DMA((2, 2, 2, 2)), reducing[-1]] + gathering[2:]
        else:
            kernel, shapes, scratch = reduce_kernel, [one], reducing
    in_vmem = pl.BlockSpec(memory_space=pltpu.VMEM)
    results = pl.pallas_call(
        kernel,
        out_shape=shapes,
        in_specs=[in_vmem] * len(given),
        out_specs=[in_vmem] * len(shapes),
        scratch_shapes=scratch,
        compiler_params=pltpu.CompilerParams(collective_id=collective_id, has_side_effects=True),
    )(*given)
    new_hidden = hidden if terms is None else results[0].reshape(rows, width)
    ready = results[-1].reshape(group * rows, width) if gather else None
    return new_hidden, ready


def on_device(candidates, in_weight, out_weight, page_cache, page_lists, hist_len):
    readers = lax.axis_size("pages")
    head_group = lax.axis_size("heads")
    layers = in_weight.shape[0]
    model_width = in_weight.shape[1]
    head_dim = out_weight.shape[2]
    pages_here = page_cache.shape[1]
    page_len = page_cache.shape[4]
    requests, max_pages = page_lists.shape
    slot_count = requests * max_pages
    capacity = 2 * slot_count // readers
    cand_rows = candidates.shape[0] * head_group
    per_request = cand_rows // requests
    history = max_pages * page_len
    score_scale = 1.0 / math.sqrt(head_dim)

    flat_ids = page_lists.reshape(slot_count)
    slot_owner = flat_ids // pages_here
    local_ids = flat_ids % pages_here
    slot_order = jnp.arange(slot_count)
    earlier_same = (slot_owner[None, :] == slot_owner[:, None]) & (
        slot_order[None, :] < slot_order[:, None]
    )
    slot_rank = jnp.sum(earlier_same.astype(jnp.int32), axis=1)
    places = slot_owner * capacity + slot_rank
    matches = places[None, :] == jnp.arange(readers * capacity)[:, None]
    asked = jnp.sum(jnp.where(matches, local_ids[None, :], 0), axis=1)
    wanted = lax.all_to_all(
        asked.reshape(readers, capacity), "pages", split_axis=0, concat_axis=0, tiled=True
    ).reshape(readers * capacity)

    def history_of(layer_index, after):
        rows = page_cache.at[layer_index, wanted, 0].get(mode="promise_in_bounds")
        rows, after = lax.optimization_barrier((rows, after))
        rows = rows.reshape((readers, capacity) + rows.shape[1:])
        return lax.all_to_all(rows, "pages", split_axis=0, concat_axis=0, tiled=True), after

    hidden_rows, ready = exchange(candidates, None, True, 0)
    history_now, ready = history_of(0, ready)
    divisors = (hist_len + 1).astype(jnp.float32)
    cand_divisors = jnp.repeat(divisors, per_request)
    live = jnp.arange(history)[None, :] < hist_len[:, None]
    for layer_index in range(layers):
        weights_in = in_weight[layer_index].reshape(model_width, 4 * head_dim)
        projected = jax.nn.silu(jnp.dot(ready, weights_in, preferred_element_type=jnp.float32))
        gate_part = projected[:, :head_dim]
        value_part = projected[:, head_dim : 2 * head_dim].astype(jnp.bfloat16)
        query_part = projected[:, 2 * head_dim : 3 * head_dim].astype(jnp.bfloat16)
        key_part = projected[:, 3 * head_dim :].astype(jnp.bfloat16)
        if layer_index + 1 < layers:
            history_next, query_part = history_of(layer_index + 1, query_part)
        got, query_part = lax.optimization_barrier((history_now, query_part))
        got = got.reshape(readers * capacity, 2, page_len, head_dim)
        listed = got.at[places].get(mode="promise_in_bounds").reshape(requests, max_pages, 2, page_len, head_dim)
        hist_keys = listed[:, :, 0].reshape(requests, history, head_dim)
        hist_values = listed[:, :, 1].reshape(requests, history, head_dim)
        queries = query_part.reshape(requests, per_request, head_dim)
        scores = (
            jnp.einsum("rqd,rtd->rqt", queries, hist_keys, preferred_element_type=jnp.float32)
            * score_scale
        )
        weights = (
            jnp.where(live[:, None, :], jax.nn.silu(scores), 0.0) / divisors[:, None, None]
        ).astype(jnp.bfloat16)
        attended = jnp.einsum(
            "rqt,rtd->rqd", weights, hist_values, preferred_element_type=jnp.float32
        ).reshape(cand_rows, head_dim)
        self_score = (
            jnp.sum(query_part.astype(jnp.float32) * key_part.astype(jnp.float32), -1) * score_scale
        )
        self_weight = (jax.nn.silu(self_score) / cand_divisors).astype(jnp.bfloat16)
        attended = attended + self_weight.astype(jnp.float32)[:, None] * value_part.astype(
            jnp.float32
        )
        gated_rows = (layer_norm(attended) * gate_part).astype(jnp.bfloat16)
        weights_out = out_weight[layer_index].reshape(head_dim, model_width)
        terms = jnp.dot(gated_rows, weights_out, preferred_element_type=jnp.float32)
        hidden_rows, ready = exchange(
            hidden_rows, terms.astype(jnp.bfloat16), layer_index + 1 < layers, layer_index + 1
        )
        history_now = history_next
    return hidden_rows


def solution(mesh):
    in_specs = (
        P(("pages", "heads"), None),
        P(None, None, "heads", None),
        P(None, "heads", None, None),
        P(None, "pages", "heads", None, None, None),
        P("pages", None),
        P("pages"),
    )
    out_specs = P(("pages", "heads"), None)
    return jax.shard_map(
        on_device, mesh=mesh, in_specs=in_specs, out_specs=out_specs, check_vma=False
    )
```

```python
import math

import jax
import jax.numpy as jnp
from jax import lax
from jax.experimental import pallas as pl
from jax.experimental.pallas import tpu as pltpu
from jax.sharding import PartitionSpec as P

eps = 1e-05


def layer_norm(values):
    row_mean = jnp.mean(values, -1, keepdims=True)
    centred = values - row_mean
    spread = jnp.mean(centred * centred, -1, keepdims=True)
    return centred * lax.rsqrt(spread + eps)


X_SIZE = 4
Z_LO = 4
Z_SIZE = 8
CORES = 2
STRIDE = 2


def heads_index(x_pos, z_hi):
    return lax.rem(x_pos + X_SIZE, X_SIZE) * 2 + z_hi


def neighbours():
    page, head = lax.axis_index("pages"), lax.axis_index("heads")
    x_pos, z_hi = head // 2, lax.rem(head, 2)
    column = page // (Z_LO * CORES)
    z_lo, core = lax.rem(page // CORES, Z_LO), lax.rem(page, CORES)

    def at_z(step):
        z_pos = lax.rem(z_hi * Z_LO + z_lo + step + Z_SIZE, Z_SIZE)
        return ((column * Z_LO + lax.rem(z_pos, Z_LO)) * CORES + core, x_pos * 2 + z_pos // Z_LO)

    return dict(
        x=x_pos,
        z=z_hi,
        right=(page, heads_index(x_pos + 1, z_hi)),
        left=(page, heads_index(x_pos - 1, z_hi)),
        up=at_z(STRIDE),
        down=at_z(-STRIDE),
    )


def greet(near):
    barrier = pltpu.get_barrier_semaphore()
    partners = [near[side] for side in ("right", "left", "up", "down")]
    for partner in partners:
        pl.semaphore_signal(
            barrier, inc=1, device_id=partner, device_id_type=pl.DeviceIdType.MESH
        )
    pl.semaphore_wait(barrier, len(partners))


def remote(source, target, sems, place, device):
    return pltpu.make_async_remote_copy(
        src_ref=source,
        dst_ref=target,
        send_sem=sems.at[(0,) + place],
        recv_sem=sems.at[(1,) + place],
        device_id=device,
        device_id_type=pl.DeviceIdType.MESH,
    )


def wide(ref_block):
    return ref_block.astype(jnp.float32)


def z_relay(near, relay, z_sems, goal):
    started = []
    for half, (ahead, behind) in enumerate((("up", "down"), ("down", "up"))):
        remote(relay.at[half], relay.at[half], z_sems, (0, half), near[behind]).wait_recv()
        leg = remote(relay.at[half], goal(near[ahead], half), z_sems, (1, half), near[ahead])
        leg.start()
        started.append(leg)
    return started


def gather_phase(near, own, out, relay, z_sems, x_sems, f_sems):
    x_pos, z_hi = near["x"], near["z"]
    mine = heads_index(x_pos, z_hi)
    started = []

    def send(copy):
        copy.start()
        started.append(copy)

    def spread(source, slot, level, half):
        for side, name in (((0, "right"), (1, "left")) if half == 0 else ((1, "left"), (0, "right"))):
            send(remote(source, out.at[slot, half], x_sems, (side, level, half), near[name]))

    def pass_on(level, z_of):
        for side, (ahead, step) in enumerate((("right", -1), ("left", 1))):
            block = out.at[heads_index(x_pos + step, z_of), side]
            remote(block, block, x_sems, (side, level, side), near[ahead]).wait_recv()
            send(remote(block, block, f_sems, (side, level), near[ahead]))

    for half, ahead in enumerate(("up", "down")):
        send(remote(own.at[half], relay.at[half], z_sems, (0, half), near[ahead]))
    for half in range(2):
        spread(own.at[half], mine, 0, half)
    out[mine] = own[...]
    pass_on(0, z_hi)

    def goal(device, half):
        return out.at[heads_index(x_pos, 1 - lax.rem(device[1], 2)), half]

    started += z_relay(near, relay, z_sems, goal)
    theirs = heads_index(x_pos, 1 - z_hi)
    for half, behind in enumerate(("down", "up")):
        block = out.at[theirs, half]
        remote(block, block, z_sems, (1, half), near[behind]).wait_recv()
        spread(block, theirs, 1, half)
    pass_on(1, 1 - z_hi)
    for level, z_of in ((0, z_hi), (1, 1 - z_hi)):
        for side, (ahead, step) in enumerate((("right", -1), ("left", 1))):
            block = out.at[heads_index(x_pos + step, z_of), 1 - side]
            remote(block, block, x_sems, (side, level, 1 - side), near[ahead]).wait_recv()
            block = out.at[heads_index(x_pos + 2, z_of), side]
            remote(block, block, f_sems, (side, level), near[ahead]).wait_recv()
    for copy in started:
        copy.wait_send()


def sum_along_x(near, terms, first, direct, joined, joined_in, x_sems):
    x_pos, z_hi = near["x"], near["z"]
    z_of = (1 - z_hi, z_hi)
    ways = ("right", "left")
    steps = (1, -1)
    started = []

    def send(copy):
        copy.start()
        started.append(copy)

    def far(level):
        for side in range(2):
            block = terms.at[heads_index(x_pos + 2, z_of[level]), side]
            send(remote(block, first.at[level, side], x_sems, (0, level, side), near[ways[side]]))

    def near_by(level):
        for side in range(2):
            block = terms.at[heads_index(x_pos + steps[side], z_of[level]), 1 - side]
            send(remote(block, direct.at[level, side], x_sems, (1, level, side), near[ways[side]]))

    def join(level):
        for side in range(2):
            here = first.at[level, side]
            remote(here, here, x_sems, (0, level, side), near[ways[side]]).wait_recv()
            own = terms[heads_index(x_pos + steps[side], z_of[level]), side]
            joined[level, side] = (wide(own) + wide(here[...])).astype(jnp.bfloat16)
            send(
                remote(
                    joined.at[level, side],
                    joined_in.at[level, side],
                    x_sems,
                    (2, level, side),
                    near[ways[side]],
                )
            )

    def total(level, half):
        here = joined_in.at[level, half]
        remote(here, here, x_sems, (2, level, half), near[ways[half]]).wait_recv()
        other = direct.at[level, 1 - half]
        remote(other, other, x_sems, (1, level, 1 - half), near[ways[1 - half]]).wait_recv()
        own = terms[heads_index(x_pos, z_of[level]), half]
        return wide(own) + wide(here[...]) + wide(other[...])

    far(0)
    near_by(0)
    far(1)
    join(0)
    near_by(1)
    join(1)
    return total, started


def reduce_phase(near, terms, first, direct, joined, joined_in, z_out, relay, z_in, z_sems, x_sems):
    total, started = sum_along_x(near, terms, first, direct, joined, joined_in, x_sems)

    def send(copy):
        copy.start()
        started.append(copy)

    for half, ahead in enumerate(("up", "down")):
        z_out[half] = total(0, half).astype(jnp.bfloat16)
        send(remote(z_out.at[half], relay.at[half], z_sems, (0, half), near[ahead]))
    sums = [total(1, half) for half in range(2)]
    started += z_relay(near, relay, z_sems, lambda device, half: z_in.at[half])
    for half, behind in enumerate(("down", "up")):
        here = z_in.at[half]
        remote(here, here, z_sems, (1, half), near[behind]).wait_recv()
        sums[half] = sums[half] + wide(here[...])
    for copy in started:
        copy.wait_send()
    return sums


def gather_kernel(hidden, out, own, *scratch):
    near = neighbours()
    for half in range(2):
        own[half] = layer_norm(wide(hidden[half])).astype(jnp.bfloat16)
    greet(near)
    gather_phase(near, own, out, *scratch)


def reduce_kernel(terms, hidden, new_hidden, *scratch):
    near = neighbours()
    greet(near)
    sums = reduce_phase(near, terms, *scratch)
    for half in range(2):
        new_hidden[half] = (wide(hidden[half]) + sums[half]).astype(jnp.bfloat16)


def reduce_gather_kernel(
    terms, hidden, new_hidden, out, first, direct, joined, joined_in,
    z_out, relay, z_in, own, z_sems, x_sems, g_sems, f_sems
):
    near = neighbours()
    greet(near)
    x_pos, z_hi = near["x"], near["z"]
    z_of = (1 - z_hi, z_hi)
    ways = (("right", -1), ("left", 1))
    total, started = sum_along_x(near, terms, first, direct, joined, joined_in, x_sems)

    def send(copy):
        copy.start()
        started.append(copy)

    for level in range(2):
        for half, ahead in enumerate(("up", "down")):
            partial = total(level, half)
            if level == 1:
                partial = partial + wide(hidden[half])
            z_out[level, half] = partial.astype(jnp.bfloat16)
            place = relay.at[level, half]
            send(remote(z_out.at[level, half], place, z_sems, (0, level, half), near[ahead]))
    for level in range(2):
        for half, (ahead, behind) in enumerate((("up", "down"), ("down", "up"))):
            place = relay.at[level, half]
            remote(place, place, z_sems, (0, level, half), near[behind]).wait_recv()
            target = z_in.at[1 - level, half]
            send(remote(place, target, z_sems, (1, level, half), near[ahead]))
    for level in (1, 0):
        slot = heads_index(x_pos, z_of[level])
        for half, behind in enumerate(("down", "up")):
            here = z_in.at[level, half]
            remote(here, here, z_sems, (1, 1 - level, half), near[behind]).wait_recv()
            rounded = (wide(z_out[level, half]) + wide(here[...])).astype(jnp.bfloat16)
            if level == 1:
                new_hidden[half] = rounded
            own[level, half] = layer_norm(wide(rounded)).astype(jnp.bfloat16)
            for side in (half, 1 - half):
                target = out.at[slot, half]
                device = near[ways[side][0]]
                send(remote(own.at[level, half], target, g_sems, (side, level, half), device))
        out[slot] = own[level]
    for level in (1, 0):
        for side, (ahead, step) in enumerate(ways):
            block = out.at[heads_index(x_pos + step, z_of[level]), side]
            remote(block, block, g_sems, (side, level, side), near[ahead]).wait_recv()
            send(remote(block, block, f_sems, (side, level), near[ahead]))
    for level in (1, 0):
        for side, (ahead, step) in enumerate(ways):
            block = out.at[heads_index(x_pos + step, z_of[level]), 1 - side]
            remote(block, block, g_sems, (side, level, 1 - side), near[ahead]).wait_recv()
            block = out.at[heads_index(x_pos + 2, z_of[level]), side]
            remote(block, block, f_sems, (side, level), near[ahead]).wait_recv()
    for copy in started:
        copy.wait_send()


def exchange(hidden, terms, gather, collective_id):
    rows, width = hidden.shape
    group = lax.axis_size("heads")
    half_rows = rows // 2
    halves = (half_rows, width)
    block = pltpu.VMEM((2,) + halves, jnp.bfloat16)
    pair = pltpu.VMEM((2, 2) + halves, jnp.bfloat16)
    gathering = [
        block,
        pltpu.SemaphoreType.DMA((2, 2, 2)),
        pltpu.SemaphoreType.DMA((2, 2, 2, 2)),
        pltpu.SemaphoreType.DMA((2, 2, 2)),
    ]
    reducing = [pair, pair, pair, pair, block, block, block]
    reducing += [pltpu.SemaphoreType.DMA((2, 2, 2)), pltpu.SemaphoreType.DMA((2, 3, 2, 2))]
    one = jax.ShapeDtypeStruct((2,) + halves, jnp.bfloat16)
    whole = jax.ShapeDtypeStruct((group, 2) + halves, jnp.bfloat16)
    if terms is None:
        kernel, shapes, scratch = gather_kernel, [whole], [block] + gathering
        given = [hidden.reshape(one.shape)]
    else:
        given = [terms.reshape(whole.shape), hidden.reshape(one.shape)]
        if gather:
            kernel, shapes = reduce_gather_kernel, [one, whole]
            scratch = [pair] * 8 + [pltpu.SemaphoreType.DMA((2, 2, 2, 2)), reducing[-1]] + gathering[2:]
        else:
            kernel, shapes, scratch = reduce_kernel, [one], reducing
    in_vmem = pl.BlockSpec(memory_space=pltpu.VMEM)
    results = pl.pallas_call(
        kernel,
        out_shape=shapes,
        in_specs=[in_vmem] * len(given),
        out_specs=[in_vmem] * len(shapes),
        scratch_shapes=scratch,
        compiler_params=pltpu.CompilerParams(collective_id=collective_id, has_side_effects=True),
    )(*given)
    new_hidden = hidden if terms is None else results[0].reshape(rows, width)
    ready = results[-1].reshape(group * rows, width) if gather else None
    return new_hidden, ready


def on_device(candidates, in_weight, out_weight, page_cache, page_lists, hist_len):
    readers = lax.axis_size("pages")
    head_group = lax.axis_size("heads")
    layers = in_weight.shape[0]
    model_width = in_weight.shape[1]
    head_dim = out_weight.shape[2]
    pages_here = page_cache.shape[1]
    page_len = page_cache.shape[4]
    requests, max_pages = page_lists.shape
    slot_count = requests * max_pages
    capacity = 2 * slot_count // readers
    cand_rows = candidates.shape[0] * head_group
    per_request = cand_rows // requests
    history = max_pages * page_len
    score_scale = 1.0 / math.sqrt(head_dim)

    flat_ids = page_lists.reshape(slot_count)
    slot_owner = flat_ids // pages_here
    local_ids = flat_ids % pages_here
    slot_order = jnp.arange(slot_count)
    earlier_same = (slot_owner[None, :] == slot_owner[:, None]) & (
        slot_order[None, :] < slot_order[:, None]
    )
    slot_rank = jnp.sum(earlier_same.astype(jnp.int32), axis=1)
    places = slot_owner * capacity + slot_rank
    matches = places[None, :] == jnp.arange(readers * capacity)[:, None]
    asked = jnp.sum(jnp.where(matches, local_ids[None, :], 0), axis=1)
    wanted = lax.all_to_all(
        asked.reshape(readers, capacity), "pages", split_axis=0, concat_axis=0, tiled=True
    ).reshape(readers * capacity)

    def history_of(layer_index, after):
        rows = page_cache.at[layer_index, wanted, 0].get(mode="promise_in_bounds")
        rows, after = lax.optimization_barrier((rows, after))
        rows = rows.reshape((readers, capacity) + rows.shape[1:])
        return lax.all_to_all(rows, "pages", split_axis=0, concat_axis=0, tiled=True), after

    hidden_rows, ready = exchange(candidates, None, True, 0)
    history_now, ready = history_of(0, ready)
    divisors = (hist_len + 1).astype(jnp.float32)
    cand_divisors = jnp.repeat(divisors, per_request)
    live = jnp.arange(history)[None, :] < hist_len[:, None]
    for layer_index in range(layers):
        weights_in = in_weight[layer_index].reshape(model_width, 4 * head_dim)
        projected = jax.nn.silu(jnp.dot(ready, weights_in, preferred_element_type=jnp.float32))
        gate_part = projected[:, :head_dim]
        value_part = projected[:, head_dim : 2 * head_dim].astype(jnp.bfloat16)
        query_part = projected[:, 2 * head_dim : 3 * head_dim].astype(jnp.bfloat16)
        key_part = projected[:, 3 * head_dim :].astype(jnp.bfloat16)
        if layer_index + 1 < layers:
            history_next, query_part = history_of(layer_index + 1, query_part)
        got, query_part = lax.optimization_barrier((history_now, query_part))
        got = got.reshape(readers * capacity, 2, page_len, head_dim)
        listed = got.at[places].get(mode="promise_in_bounds").reshape(requests, max_pages, 2, page_len, head_dim)
        hist_keys = listed[:, :, 0].reshape(requests, history, head_dim)
        hist_values = listed[:, :, 1].reshape(requests, history, head_dim)
        queries = query_part.reshape(requests, per_request, head_dim)
        scores = (
            jnp.einsum("rqd,rtd->rqt", queries, hist_keys, preferred_element_type=jnp.float32)
            * score_scale
        )
        weights = (
            jnp.where(live[:, None, :], jax.nn.silu(scores), 0.0) / divisors[:, None, None]
        ).astype(jnp.bfloat16)
        attended = jnp.einsum(
            "rqt,rtd->rqd", weights, hist_values, preferred_element_type=jnp.float32
        ).reshape(cand_rows, head_dim)
        self_score = (
            jnp.sum(query_part.astype(jnp.float32) * key_part.astype(jnp.float32), -1) * score_scale
        )
        self_weight = (jax.nn.silu(self_score) / cand_divisors).astype(jnp.bfloat16)
        attended = attended + self_weight.astype(jnp.float32)[:, None] * value_part.astype(
            jnp.float32
        )
        gated_rows = (layer_norm(attended) * gate_part).astype(jnp.bfloat16)
        weights_out = out_weight[layer_index].reshape(head_dim, model_width)
        terms = jnp.dot(gated_rows, weights_out, preferred_element_type=jnp.float32)
        hidden_rows, ready = exchange(
            hidden_rows, terms.astype(jnp.bfloat16), layer_index + 1 < layers, layer_index + 1
        )
        history_now = history_next
    return hidden_rows


def solution(mesh):
    in_specs = (
        P(("pages", "heads"), None),
        P(None, None, "heads", None),
        P(None, "heads", None, None),
        P(None, "pages", "heads", None, None, None),
        P("pages", None),
        P("pages"),
    )
    out_specs = P(("pages", "heads"), None)
    return jax.shard_map(
        on_device, mesh=mesh, in_specs=in_specs, out_specs=out_specs, check_vma=False
    )
```
